512 devices in a mesh: segment: 4 (over x), graph: 128 (over y, z, core).
Axes of the slice: x: 4, y: 8, z: 8, core: 2. Of those that a mesh axis runs over, the one named last changes fastest.
Arguments:
- features: bfloat16 [65536, 1024], P('graph'), may hold values from -6 to 6
- weights: bfloat16 [8, 1024, 1024], P(None, 'graph'), may hold values from -0.75 to 0.75
- history: bfloat16 [8, 8192, 1024], P(None, 'graph'), may hold values from 0 to 1.1953125
- own_adj: bfloat16 [4, 16384, 128], P(None, 'graph'), may hold values from 0 to 0.00390625
- side_adj: bfloat16 [4, 4, 2048, 128], P(None, None, 'graph'), may hold values from 0 to 0.012451172
- hist_adj: bfloat16 [4, 8192, 128], P(None, 'graph'), may hold values from 0 to 0.009338379
- send_ids: int32 [4, 4, 2048], P(None, None, 'graph'), may hold values from 0 to 127, as said below
- hist_ids: int32 [4, 8192], P(None, 'graph'), may hold values from 0 to 63
Outputs:
- layer_out: bfloat16 [8, 65536, 1024], P('segment', 'graph')
The draws below stay inside these ranges and needn't reach their ends.
Inputs may be any that keep to these rules, and one draw needn't show every extreme that they name: `send_ids`: each list of 16 row numbers for one batch, one partition and one direction has distinct entries.
All inputs are finite; a program needn't handle non-finite values.
Results may differ from the reference program's by a relative error of at most 0.0032.
Values may be sent and summed in bfloat16 or wider, within the bound.
No kernel may reach another device: no remote copies, remote signals or barrier semaphores. Data moves between devices by JAX's collectives and lax.ppermute only.
A program may use at most 64 MiB of HBM per device.

```python
import jax
import jax.numpy as jnp

F = 1024
LAYERS = 8
BATCHES = 4
BR = 128
EDGE_ROWS = 16
HIST_SEL = 64
HIST_ROWS = 64
VERTS = 65536
BR_ALL = 16384
SEND_ALL = 2048
HSEL_ALL = 8192
HIST_ALL = 8192
N_GRAPH = 128


def draw_send_ids(key, part):
    list_count = BATCHES * 4 * (SEND_ALL // EDGE_ROWS)
    subkeys = jax.random.split(jax.random.fold_in(key, 7), list_count)
    chosen = jax.vmap(lambda single: jax.random.permutation(single, BR)[:EDGE_ROWS])(subkeys)
    return chosen.astype(jnp.int32).reshape(BATCHES, 4, SEND_ALL)


def place_ends(result, own_key, low, largest):
    place = [jax.random.randint(jax.random.fold_in(own_key, axis), (), 0, length) for axis, length in enumerate(result.shape)]
    widest = result.shape.index(max(result.shape))
    neighbour = place[:widest] + [(place[widest] + 1) % result.shape[widest]] + place[widest + 1:]
    return result.at[tuple(place)].set(low).at[tuple(neighbour)].set(largest)


def with_spikes(drawn, stream_key, source, target, blocks, factor):
    def block_of(axis_at):
        return (jnp.arange(drawn.shape[axis_at]) // (drawn.shape[axis_at] // blocks)).reshape((-1,) + (1,) * (drawn.ndim - 1 - axis_at))

    first = jax.random.permutation(stream_key, blocks)[block_of(target)]
    second = (block_of(target) + blocks // 2) % blocks
    return jnp.where((block_of(source) == first) | (block_of(source) == second), factor * drawn, drawn)


def shard_levels(stream_key, dims, cuts, smallest, high):
    def one(axis_at, shards_of):
        heights = jax.random.uniform(jax.random.fold_in(jax.random.fold_in(stream_key, 6), axis_at), (shards_of,), jnp.float32, smallest / len(cuts), high / len(cuts))
        return jnp.repeat(jnp.exp(heights), dims[axis_at] // shards_of).reshape((-1,) + (1,) * (len(dims) - axis_at - 1))

    loudness = one(*cuts[0])
    for cut in cuts[1:]:
        loudness = loudness * one(*cut)
    return loudness


def noise(rng, extent, width, reach, pieces=(), kind=jnp.bfloat16):
    array = width * jax.random.normal(rng, extent, jnp.float32)
    if pieces:
        array = array * shard_levels(rng, extent, pieces, -0.22, 0.18)
    return jnp.clip(array, -reach, reach).astype(kind)


def gaussian_with(own_key, extent, width, most, cuts, heavy, kind=jnp.bfloat16):
    entries = width * jax.random.normal(own_key, extent, jnp.float32)
    if cuts:
        entries = entries * shard_levels(own_key, extent, cuts, -0.22, 0.18)
    return jnp.clip(with_spikes(entries, jax.random.fold_in(own_key, 3), *heavy), -most, most).astype(kind)


def setup_inputs(seed: int = 0) -> dict:
    arg_keys = jax.random.split(jax.random.key(seed), 9)
    features = noise(arg_keys[0], (VERTS, F), 1.0, 6.0, ((0, 128),))
    weights = gaussian_with(arg_keys[1], (LAYERS, F, F), F ** -0.5, 0.75, ((1, 128),), (1, 2, 128, 5.5))
    history = jnp.clip(1.1953125 * jax.random.uniform(arg_keys[2], (LAYERS, HIST_ALL, F), jnp.float32) ** shard_levels(arg_keys[2], (LAYERS, HIST_ALL, F), ((1, 128),), -0.2, 0.2), 0.0, 1.1953125).astype(jnp.bfloat16)
    own_adj = jnp.clip(0.00390625 * jax.random.uniform(arg_keys[3], (BATCHES, BR_ALL, BR), jnp.float32) ** shard_levels(arg_keys[3], (BATCHES, BR_ALL, BR), ((1, 128),), -0.2, 0.2), 0.0, 0.00390625).astype(jnp.bfloat16)
    side_adj = jnp.clip(0.012451172 * jax.random.uniform(arg_keys[4], (BATCHES, 4, SEND_ALL, BR), jnp.float32) ** shard_levels(arg_keys[4], (BATCHES, 4, SEND_ALL, BR), ((2, 128),), -0.2, 0.2), 0.0, 0.012451172).astype(jnp.bfloat16)
    hist_adj = jnp.clip(0.009338379 * jax.random.uniform(arg_keys[5], (BATCHES, HSEL_ALL, BR), jnp.float32) ** shard_levels(arg_keys[5], (BATCHES, HSEL_ALL, BR), ((1, 128),), -0.2, 0.2), 0.0, 0.009338379).astype(jnp.bfloat16)
    send_ids = draw_send_ids(jax.random.fold_in(arg_keys[8], 71), 0)
    hist_ids = place_ends(jax.random.randint(arg_keys[7], (BATCHES, HSEL_ALL), 0, HIST_ROWS), jax.random.fold_in(arg_keys[7], 1), 0, HIST_ROWS - 1).astype(jnp.int32)
    return dict(features=features, weights=weights, history=history, own_adj=own_adj, side_adj=side_adj, hist_adj=hist_adj, send_ids=send_ids, hist_ids=hist_ids)


ALPHA = 0.1
LAMBDA = 1.5
OFFSETS = (1, -1, 2, -2)


def displace(blocks, offset):
    padding = jnp.zeros((abs(offset),) + blocks.shape[1:], blocks.dtype)
    if offset > 0:
        return jnp.concatenate([padding, blocks[:-offset]], axis=0)
    return jnp.concatenate([blocks[-offset:], padding], axis=0)


def layer_step(current, initial, number, weight, tables, own_tile, side_tile, hist_tile, send_rows, past_rows):
    aggregate = jnp.einsum("pij,pjf->pif", own_tile.astype(jnp.float32), current.astype(jnp.float32))
    picked = jax.vmap(lambda source, chosen: source[chosen])(current, send_rows)
    for direction in range(4):
        arrived = displace(picked[:, direction], OFFSETS[direction])
        aggregate = aggregate + jnp.einsum("pri,prf->pif", side_tile[direction].astype(jnp.float32), arrived.astype(jnp.float32))
    looked = jax.vmap(lambda source, chosen: source[chosen])(tables[number], past_rows)
    aggregate = aggregate + jnp.einsum("pri,prf->pif", hist_tile.astype(jnp.float32), looked.astype(jnp.float32))
    support = (1.0 - ALPHA) * aggregate + ALPHA * initial.astype(jnp.float32)
    columns = support.shape[2]
    mixing = jnp.dot(support.astype(jnp.bfloat16).reshape(-1, columns), weight, preferred_element_type=jnp.float32).reshape(support.shape)
    strength = jnp.log(LAMBDA / (jnp.float32(number) + 1.0) + 1.0)
    return jax.nn.relu((1.0 - strength) * support + strength * mixing).astype(jnp.bfloat16)


def reference(features, weights, history, own_adj, side_adj, hist_adj, send_ids, hist_ids):
    columns = features.shape[1]
    inputs = features.reshape(N_GRAPH, BATCHES, BR, columns)
    tables = history.reshape(LAYERS, N_GRAPH, HIST_ROWS, columns)
    own_all = own_adj.reshape(BATCHES, N_GRAPH, BR, BR)
    side_all = side_adj.reshape(BATCHES, 4, N_GRAPH, EDGE_ROWS, BR)
    hist_all = hist_adj.reshape(BATCHES, N_GRAPH, HIST_SEL, BR)
    send_all = send_ids.reshape(BATCHES, 4, N_GRAPH, EDGE_ROWS).transpose(0, 2, 1, 3)
    past_all = hist_ids.reshape(BATCHES, N_GRAPH, HIST_SEL)
    collected = []
    for batch in range(BATCHES):
        initial = inputs[:, batch]
        current = initial
        produced = []
        for number in range(LAYERS):
            current = layer_step(current, initial, number, weights[number], tables, own_all[batch], side_all[batch], hist_all[batch], send_all[batch], past_all[batch])
            produced.append(current)
        collected.append(jnp.stack(produced))
    stacked = jnp.stack(collected, axis=1)
    return stacked.transpose(0, 2, 1, 3, 4).reshape(LAYERS, N_GRAPH * BATCHES * BR, columns)
```

```python
import jax
import jax.numpy as jnp
from jax import lax
from jax.sharding import PartitionSpec as P

ALPHA = 0.1
LAMBDA = 1.5
BF = jnp.bfloat16
F32 = jnp.float32


def dot(a, b):
    return jnp.dot(a, b, preferred_element_type=F32)


def dot_t(a, b):
    return lax.dot_general(a, b, (((0,), (0,)), ((), ())), preferred_element_type=F32)


def one_hot(ids, width):
    return (ids[:, None] == lax.broadcasted_iota(jnp.int32, (ids.shape[0], width), 1)).astype(BF)


def shards(features, weights, history, own_adj, side_adj, hist_adj, send_ids, hist_ids):
    segment_pos = lax.axis_index("segment")
    segment_count = lax.axis_size("segment")
    graph_count = lax.axis_size("graph")
    core = lax.axis_index("graph") % 2
    layers, wrows, width = weights.shape
    half = width // 2
    rows = own_adj.shape[2]
    edge = send_ids.shape[2]
    hsel = hist_ids.shape[1]
    kept = layers // segment_count

    def partner(value):
        return lax.ppermute(value, "graph", [(p, p ^ 1) for p in range(graph_count)])

    def chip_shift(value, step):
        low, high = max(0, -step), min(graph_count, graph_count - step)
        return lax.ppermute(value, "graph", [(p, p + step) for p in range(low, high)])

    def pick_batch(value):
        return lax.dynamic_index_in_dim(value, segment_pos, 0, keepdims=False)

    def mine_half(value):
        return jnp.where(core == 0, value[..., :half], value[..., half:])

    def other_half(value):
        return jnp.where(core == 0, value[..., half:], value[..., :half])

    def by_part(mine, theirs):
        return jnp.where(core == 0, mine, theirs), jnp.where(core == 0, theirs, mine)

    w_swapped = partner(other_half(weights))
    w_low, w_high = by_part(mine_half(weights), w_swapped)
    w_chip = jnp.concatenate([w_low, w_high], axis=1)
    groups = [[p for p in range(graph_count) if p % 2 == c] for c in range(2)]

    initial = lax.dynamic_slice_in_dim(features, segment_pos * rows, rows, 0)
    own = pick_batch(own_adj)
    side = pick_batch(side_adj).reshape(4 * edge, rows)
    hist = pick_batch(hist_adj)
    sids = pick_batch(send_ids).reshape(-1)
    hids = pick_batch(hist_ids)
    x0, x1 = by_part(mine_half(initial), partner(other_half(initial)))
    h0, h1 = by_part(mine_half(history), partner(other_half(history)))
    tables = jnp.concatenate([own, side, hist], axis=0)
    t0, t1 = by_part(tables, partner(tables))
    ids = jnp.concatenate([sids, hids])
    i0, i1 = by_part(ids, partner(ids))

    def split(t, i):
        own = t[:rows]
        side = [t[rows + k * edge : rows + (k + 1) * edge] for k in range(4)]
        hist = t[rows + 4 * edge :]
        send = [one_hot(i[k * edge : (k + 1) * edge], rows) for k in range(4)]
        look = one_hot(i[4 * edge :], history.shape[1])
        return own, side, hist, send, look

    own0, side0, hist0, send0, look0 = split(t0, i0)
    own1, side1, hist1, send1, look1 = split(t1, i1)
    q10 = dot_t(side1[0], send0[0]).astype(BF)
    q01 = dot_t(side0[1], send1[1]).astype(BF)
    near = jnp.concatenate(
        [jnp.concatenate([own0, q01], axis=1), jnp.concatenate([q10, own1], axis=1)], axis=0
    )
    zs = jnp.zeros_like(side0[0])
    far_t = jnp.concatenate(
        [
            jnp.concatenate([side0[0], side0[2], zs, side0[3], zs, zs], axis=0),
            jnp.concatenate([zs, zs, side1[2], zs, side1[1], side1[3]], axis=0),
        ],
        axis=1,
    )
    zp = jnp.zeros_like(send0[0])
    picker = jnp.concatenate(
        [
            jnp.concatenate([zp, send1[0]], axis=1),
            jnp.concatenate([send0[2], zp], axis=1),
            jnp.concatenate([zp, send1[2]], axis=1),
            jnp.concatenate([send0[3], zp], axis=1),
            jnp.concatenate([send0[1], zp], axis=1),
            jnp.concatenate([zp, send1[3]], axis=1),
        ],
        axis=0,
    )
    start = jnp.concatenate([x0, x1], axis=0)
    start32 = ALPHA * start.astype(F32)

    def past(layer):
        g0 = dot(look0, h0[layer]).astype(BF)
        g1 = dot(look1, h1[layer]).astype(BF)
        return jnp.concatenate([dot_t(hist0, g0), dot_t(hist1, g1)], axis=0)

    weight_parts = []
    for layer in range(0, layers, 2):
        shard = w_chip[layer : layer + 2].reshape(2, 2 * wrows, half)
        full = lax.all_gather(shard, "graph", axis=1, tiled=True, axis_index_groups=groups)
        weight_parts += [full[0], full[1]]

    current = start
    own_rows = []
    for layer in range(layers):
        strength = jnp.log(jnp.float32(LAMBDA / (layer + 1.0)) + 1.0)
        picked = dot(picker, current).astype(BF)
        before = chip_shift(picked[: 3 * edge], 2)
        after = chip_shift(picked[3 * edge :], -2)
        local = dot(near, current) + past(layer)
        arrived = jnp.concatenate([before, after], axis=0)
        support = (1.0 - ALPHA) * (local + dot_t(far_t, arrived)) + start32
        mine = support.astype(BF)
        theirs = partner(mine)
        left, right = by_part(mine, theirs)
        weight = weight_parts[layer]
        mixing = dot(left, weight[:half]) + dot(right, weight[half:])
        current = jax.nn.relu((1.0 - strength) * support + strength * mixing).astype(BF)
        own_rows.append(current)
    stacked = jnp.stack(own_rows).reshape(layers, 2, rows, half)
    to_keep = jnp.where(core == 0, stacked[:, 0], stacked[:, 1])
    to_send = jnp.where(core == 0, stacked[:, 1], stacked[:, 0])
    left, right = by_part(to_keep, partner(to_send))
    whole = jnp.concatenate([left, right], axis=2).reshape(segment_count, kept, rows, width)
    exchanged = lax.all_to_all(whole, "segment", 0, 0)
    return exchanged.transpose(1, 0, 2, 3).reshape(kept, segment_count * rows, width)


def solution(mesh):
    in_specs = (
        P("graph", None),
        P(None, "graph", None),
        P(None, "graph", None),
        P(None, "graph", None),
        P(None, None, "graph", None),
        P(None, "graph", None),
        P(None, None, "graph"),
        P(None, "graph"),
    )
    out_specs = P("segment", "graph", None)
    return jax.shard_map(shards, mesh=mesh, in_specs=in_specs, out_specs=out_specs, check_vma=False)
```

```python
import jax
import jax.numpy as jnp
from jax import lax
from jax.sharding import PartitionSpec as P

ALPHA = 0.1
LAMBDA = 1.5
BF = jnp.bfloat16
F32 = jnp.float32


def dot(a, b):
    return jnp.dot(a, b, preferred_element_type=F32)


def dot_t(a, b):
    return lax.dot_general(a, b, (((0,), (0,)), ((), ())), preferred_element_type=F32)


def one_hot(ids, width):
    return (ids[:, None] == lax.broadcasted_iota(jnp.int32, (ids.shape[0], width), 1)).astype(BF)


def shards(features, weights, history, own_adj, side_adj, hist_adj, send_ids, hist_ids):
    segment_pos = lax.axis_index("segment")
    segment_count = lax.axis_size("segment")
    graph_count = lax.axis_size("graph")
    core = lax.axis_index("graph") % 2
    chip_odd = (lax.axis_index("graph") // 2) % 2
    layers, _, width = weights.shape
    rows = own_adj.shape[2]
    edge = send_ids.shape[2]
    kept = layers // segment_count
    resident = lax.all_gather(weights, "graph", axis=1, tiled=True)

    def partner(value):
        return lax.ppermute(value, "graph", [(p, p ^ 1) for p in range(graph_count)])

    def exchange(value, first):
        pairs = []
        for p in range(first, graph_count - first - 2, 4):
            for c in range(2):
                pairs += [(p + c, p + c + 2), (p + c + 2, p + c)]
        return lax.ppermute(value, "graph", pairs)

    def pick_batch(value):
        return lax.dynamic_index_in_dim(value, segment_pos, 0, keepdims=False)

    def by_part(mine, theirs):
        return jnp.where(core == 0, mine, theirs), jnp.where(core == 0, theirs, mine)

    initial = lax.dynamic_slice_in_dim(features, segment_pos * rows, rows, 0)
    own = pick_batch(own_adj)
    side = pick_batch(side_adj).reshape(4 * edge, rows)
    hist = pick_batch(hist_adj)
    sids = pick_batch(send_ids).reshape(-1)
    hids = pick_batch(hist_ids)
    tables = jnp.concatenate([own, side, hist], axis=0)
    ids = jnp.concatenate([sids, hids])
    i0, i1 = by_part(ids, partner(ids))
    t0, t1 = by_part(tables, partner(tables))
    x0, x1 = by_part(initial, partner(initial))

    looked = jax.vmap(lambda t: dot(one_hot(hids, t.shape[0]), t).astype(BF))(history)
    g0, g1 = by_part(looked, partner(looked))

    def split(t, i):
        own = t[:rows]
        side = [t[rows + k * edge : rows + (k + 1) * edge] for k in range(4)]
        hist = t[rows + 4 * edge :]
        send = [one_hot(i[k * edge : (k + 1) * edge], rows) for k in range(4)]
        return own, side, hist, send

    own0, side0, hist0, send0 = split(t0, i0)
    own1, side1, hist1, send1 = split(t1, i1)
    q10 = dot_t(side1[0], send0[0]).astype(BF)
    q01 = dot_t(side0[1], send1[1]).astype(BF)
    near = jnp.concatenate(
        [jnp.concatenate([own0, q01], axis=1), jnp.concatenate([q10, own1], axis=1)], axis=0
    )
    zs = jnp.zeros_like(side0[0])
    from_before = jnp.concatenate(
        [
            jnp.concatenate([side0[0], side0[2], zs], axis=0),
            jnp.concatenate([zs, zs, side1[2]], axis=0),
        ],
        axis=1,
    )
    from_after = jnp.concatenate(
        [
            jnp.concatenate([side0[3], zs, zs], axis=0),
            jnp.concatenate([zs, side1[1], side1[3]], axis=0),
        ],
        axis=1,
    )
    to_after = jnp.concatenate(
        [
            jnp.concatenate([zs, send1[0]], axis=1),
            jnp.concatenate([send0[2], zs], axis=1),
            jnp.concatenate([zs, send1[2]], axis=1),
        ],
        axis=0,
    )
    to_before = jnp.concatenate(
        [
            jnp.concatenate([send0[3], zs], axis=1),
            jnp.concatenate([send0[1], zs], axis=1),
            jnp.concatenate([zs, send1[3]], axis=1),
        ],
        axis=0,
    )
    far_a = jnp.where(chip_odd == 0, from_after, from_before)
    far_b = jnp.where(chip_odd == 0, from_before, from_after)
    pick_a = jnp.where(chip_odd == 0, to_after, to_before)
    pick_b = jnp.where(chip_odd == 0, to_before, to_after)
    zh = jnp.zeros_like(hist0)
    hist_t = jnp.concatenate(
        [jnp.concatenate([hist0, zh], axis=1), jnp.concatenate([zh, hist1], axis=1)], axis=0
    )
    looked = jnp.concatenate([g0, g1], axis=1)
    start = jnp.concatenate([x0, x1], axis=0)

    current = start
    own_rows = []
    for layer in range(layers):
        strength = jnp.log(jnp.float32(LAMBDA / (layer + 1.0)) + 1.0)
        got_a = exchange(dot(pick_a, current).astype(BF), 0)
        got_b = exchange(dot(pick_b, current).astype(BF), 2)
        local = dot(near, current) + dot_t(hist_t, looked[layer])
        total = local + dot_t(far_a, got_a) + dot_t(far_b, got_b)
        support = (1.0 - ALPHA) * total + ALPHA * start.astype(F32)
        mixing = dot(support.astype(BF), resident[layer])
        current = jax.nn.relu((1.0 - strength) * support + strength * mixing).astype(BF)
        own_rows.append(lax.dynamic_slice_in_dim(current, core * rows, rows, 0))
    whole = jnp.stack(own_rows).reshape(segment_count, kept, rows, width)
    exchanged = lax.all_to_all(whole, "segment", 0, 0)
    return exchanged.transpose(1, 0, 2, 3).reshape(kept, segment_count * rows, width)


def solution(mesh):
    in_specs = (
        P("graph", None),
        P(None, "graph", None),
        P(None, "graph", None),
        P(None, "graph", None),
        P(None, None, "graph", None),
        P(None, "graph", None),
        P(None, None, "graph"),
        P(None, "graph"),
    )
    out_specs = P("segment", "graph", None)
    return jax.shard_map(shards, mesh=mesh, in_specs=in_specs, out_specs=out_specs, check_vma=False)
```

```python
import jax
import jax.numpy as jnp
from jax import lax
from jax.experimental import pallas as pl
from jax.experimental.pallas import tpu as pltpu
from jax.sharding import PartitionSpec as P

ALPHA = 0.1
LAMBDA = 1.5
BF = jnp.bfloat16
F32 = jnp.float32


def dot(a, b):
    return jnp.dot(a, b, preferred_element_type=F32)


def dot_t(a, b):
    return lax.dot_general(a, b, (((0,), (0,)), ((), ())), preferred_element_type=F32)


def one_hot(ids, width):
    return (ids[:, None] == lax.broadcasted_iota(jnp.int32, (ids.shape[0], width), 1)).astype(BF)


VM = pl.BlockSpec(memory_space=pltpu.VMEM)
HB = pl.BlockSpec(memory_space=pltpu.HBM)


def in_vmem(*values):
    return [pltpu.with_memory_space_constraint(v, pltpu.VMEM) for v in values]


def finish_body(layer, strip, prefetched, *refs):
    if prefetched:
        local, got_a, got_b, far, picks, start, weight, new, out_a, out_b, total, rounded = refs
    else:
        local, got_a, got_b, far, picks, start, stored = refs[:7]
        new, out_a, out_b, total, rounded, weight, sem = refs[7:]
        copy = pltpu.make_async_copy(stored.at[layer], weight, sem)
        copy.start()
    width = start.shape[1]
    edges = got_a.shape[0]
    strength = jnp.log(jnp.float32(LAMBDA / (layer + 1.0)) + 1.0)
    for low in range(0, width, strip):
        cols = slice(low, low + strip)
        got = jnp.concatenate([got_a[:, cols], got_b[:, cols]], axis=0)
        summed = local[:, cols] + dot(far[...], got)
        support = (1.0 - ALPHA) * summed + ALPHA * start[:, cols].astype(F32)
        total[:, cols] = support
        rounded[:, cols] = support.astype(BF)
    if not prefetched:
        copy.wait()
    for low in range(0, width, strip):
        cols = slice(low, low + strip)
        mixing = dot(rounded[...], weight[:, cols])
        fresh = jax.nn.relu((1.0 - strength) * total[:, cols] + strength * mixing).astype(BF)
        new[:, cols] = fresh
        sent = dot(picks[...], fresh).astype(BF)
        out_a[:, cols] = sent[:edges]
        out_b[:, cols] = sent[edges:]


def finish(layer, local, got_a, got_b, far, picks, start, weight, prefetched):
    rows, width = start.shape
    edges = got_a.shape[0]
    ins = in_vmem(local, got_a, got_b, far, picks, start)
    scratch = [pltpu.VMEM((rows, width), F32), pltpu.VMEM((rows, width), BF)]
    if prefetched:
        ins += in_vmem(weight)
    else:
        ins.append(pltpu.with_memory_space_constraint(weight, pltpu.HBM))
        scratch += [pltpu.VMEM(weight.shape[1:], BF), pltpu.SemaphoreType.DMA]
    return pl.pallas_call(
        lambda *refs: finish_body(layer, min(256, width), prefetched, *refs),
        out_shape=(
            pltpu.VMEM((rows, width), BF),
            pltpu.VMEM((edges, width), BF),
            pltpu.VMEM((edges, width), BF),
        ),
        in_specs=[VM] * 6 + [VM if prefetched else HB],
        out_specs=(VM, VM, VM),
        scratch_shapes=scratch,
        compiler_params=pltpu.CompilerParams(vmem_limit_bytes=10 << 20),
        name="finish",
    )(*ins)


def begin_body(layer, strip, *refs):
    if layer is None:
        current, near, hist, looked, local = refs
    else:
        current, near, hist, looked, stored, local, weight, sem = refs
        copy = pltpu.make_async_copy(stored.at[layer], weight, sem)
        copy.start()
    for low in range(0, current.shape[1], strip):
        cols = slice(low, low + strip)
        local[:, cols] = dot(near[...], current[:, cols]) + dot(hist[...], looked[:, cols])
    if layer is not None:
        copy.wait()


def begin(layer, current, near, hist, looked, stored):
    rows, width = current.shape
    ins = in_vmem(current, near, hist, looked)
    outs = [pltpu.VMEM((rows, width), F32)]
    scratch = []
    if layer is not None:
        ins.append(pltpu.with_memory_space_constraint(stored, pltpu.HBM))
        outs.append(pltpu.VMEM(stored.shape[1:], BF))
        scratch.append(pltpu.SemaphoreType.DMA)
    return pl.pallas_call(
        lambda *refs: begin_body(layer, min(256, width), *refs),
        out_shape=tuple(outs),
        in_specs=[VM] * 4 + [HB] * (layer is not None),
        out_specs=(VM,) * len(outs),
        scratch_shapes=scratch,
        compiler_params=pltpu.CompilerParams(vmem_limit_bytes=4 << 20),
        name="begin",
    )(*ins)


def shards(features, weights, history, own_adj, side_adj, hist_adj, send_ids, hist_ids):
    segment_pos = lax.axis_index("segment")
    segment_count = lax.axis_size("segment")
    graph_count = lax.axis_size("graph")
    core = lax.axis_index("graph") % 2
    chip_odd = (lax.axis_index("graph") // 2) % 2
    layers, _, width = weights.shape
    rows = own_adj.shape[2]
    edge = send_ids.shape[2]
    kept = layers // segment_count
    resident = lax.all_gather(weights, "graph", axis=1, tiled=True)

    def partner(value):
        return lax.ppermute(value, "graph", [(p, p ^ 1) for p in range(graph_count)])

    def exchange(value, first):
        pairs = []
        for p in range(first, graph_count - first - 2, 4):
            for c in range(2):
                pairs += [(p + c, p + c + 2), (p + c + 2, p + c)]
        return lax.ppermute(value, "graph", pairs)

    def pick_batch(value):
        return lax.dynamic_index_in_dim(value, segment_pos, 0, keepdims=False)

    def by_part(mine, theirs):
        return jnp.where(core == 0, mine, theirs), jnp.where(core == 0, theirs, mine)

    initial = lax.dynamic_slice_in_dim(features, segment_pos * rows, rows, 0)
    own = pick_batch(own_adj)
    side = pick_batch(side_adj).reshape(4 * edge, rows)
    hist = pick_batch(hist_adj)
    sids = pick_batch(send_ids).reshape(-1)
    hids = pick_batch(hist_ids)
    tables = jnp.concatenate([own, side, hist], axis=0)
    ids = jnp.concatenate([sids, hids])
    i0, i1 = by_part(ids, partner(ids))
    t0, t1 = by_part(tables, partner(tables))
    x0, x1 = by_part(initial, partner(initial))

    looked = jax.vmap(lambda t: dot(one_hot(hids, t.shape[0]), t).astype(BF))(history)
    g0, g1 = by_part(looked, partner(looked))

    def split(t, i):
        own = t[:rows]
        side = [t[rows + k * edge : rows + (k + 1) * edge] for k in range(4)]
        hist = t[rows + 4 * edge :]
        send = [one_hot(i[k * edge : (k + 1) * edge], rows) for k in range(4)]
        return own, side, hist, send

    own0, side0, hist0, send0 = split(t0, i0)
    own1, side1, hist1, send1 = split(t1, i1)
    q10 = dot_t(side1[0], send0[0]).astype(BF)
    q01 = dot_t(side0[1], send1[1]).astype(BF)
    near = jnp.concatenate(
        [jnp.concatenate([own0, q01], axis=1), jnp.concatenate([q10, own1], axis=1)], axis=0
    )
    zs = jnp.zeros_like(side0[0])
    from_before = jnp.concatenate(
        [
            jnp.concatenate([side0[0], side0[2], zs], axis=0),
            jnp.concatenate([zs, zs, side1[2]], axis=0),
        ],
        axis=1,
    )
    from_after = jnp.concatenate(
        [
            jnp.concatenate([side0[3], zs, zs], axis=0),
            jnp.concatenate([zs, side1[1], side1[3]], axis=0),
        ],
        axis=1,
    )
    to_after = jnp.concatenate(
        [
            jnp.concatenate([zs, send1[0]], axis=1),
            jnp.concatenate([send0[2], zs], axis=1),
            jnp.concatenate([zs, send1[2]], axis=1),
        ],
        axis=0,
    )
    to_before = jnp.concatenate(
        [
            jnp.concatenate([send0[3], zs], axis=1),
            jnp.concatenate([send0[1], zs], axis=1),
            jnp.concatenate([zs, send1[3]], axis=1),
        ],
        axis=0,
    )
    far_a = jnp.where(chip_odd == 0, from_after, from_before)
    far_b = jnp.where(chip_odd == 0, from_before, from_after)
    pick_a = jnp.where(chip_odd == 0, to_after, to_before)
    pick_b = jnp.where(chip_odd == 0, to_before, to_after)
    zh = jnp.zeros_like(hist0)
    hist_t = jnp.concatenate(
        [jnp.concatenate([hist0, zh], axis=1), jnp.concatenate([zh, hist1], axis=1)], axis=0
    )
    looked = jnp.concatenate([g0, g1], axis=1)
    start = jnp.concatenate([x0, x1], axis=0)

    far = jnp.concatenate([far_a, far_b], axis=0).T
    picks = jnp.concatenate([pick_a, pick_b], axis=0)
    hist_n = hist_t.T
    current = start
    sent = dot(picks, current).astype(BF)
    send_a, send_b = sent[: 3 * edge], sent[3 * edge :]
    (local,) = begin(None, current, near, hist_n, looked[0], None)
    weight = resident
    own_rows = []
    for layer in range(layers):
        got_a = exchange(send_a, 0)
        got_b = exchange(send_b, 2)
        current, send_a, send_b = finish(
            layer, local, got_a, got_b, far, picks, start, weight, layer > 0
        )
        if layer + 1 < layers:
            local, weight = begin(layer + 1, current, near, hist_n, looked[layer + 1], resident)
        own_rows.append(lax.dynamic_slice_in_dim(current, core * rows, rows, 0))
    whole = jnp.stack(own_rows)
    return lax.all_to_all(whole, "segment", 0, 1, tiled=True)


def solution(mesh):
    in_specs = (
        P("graph", None),
        P(None, "graph", None),
        P(None, "graph", None),
        P(None, "graph", None),
        P(None, None, "graph", None),
        P(None, "graph", None),
        P(None, None, "graph"),
        P(None, "graph"),
    )
    out_specs = P("segment", "graph", None)
    return jax.shard_map(shards, mesh=mesh, in_specs=in_specs, out_specs=out_specs, check_vma=False)
```

```python
import jax
import jax.numpy as jnp
from jax import lax
from jax.experimental import pallas as pl
from jax.experimental.pallas import tpu as pltpu
from jax.sharding import PartitionSpec as P

ALPHA = 0.1
LAMBDA = 1.5
BF = jnp.bfloat16
F32 = jnp.float32


def dot(a, b):
    return jnp.dot(a, b, preferred_element_type=F32)


def dot_t(a, b):
    return lax.dot_general(a, b, (((0,), (0,)), ((), ())), preferred_element_type=F32)


def one_hot(ids, width):
    return (ids[:, None] == lax.broadcasted_iota(jnp.int32, (ids.shape[0], width), 1)).astype(BF)


VM = pl.BlockSpec(memory_space=pltpu.VMEM)
HB = pl.BlockSpec(memory_space=pltpu.HBM)
SM = pl.BlockSpec(memory_space=pltpu.SMEM)
EARLY = 2


def in_vmem(*values):
    return [pltpu.with_memory_space_constraint(v, pltpu.VMEM) for v in values]


def add_up(strip, local, got_a, got_b, far, start, total, rounded):
    for low in range(0, start.shape[1], strip):
        cols = slice(low, low + strip)
        got = jnp.concatenate([got_a[:, cols], got_b[:, cols]], axis=0)
        summed = local[:, cols] + dot(far[...], got)
        support = (1.0 - ALPHA) * summed + ALPHA * start[:, cols].astype(F32)
        total[:, cols] = support
        rounded[:, cols] = support.astype(BF)


def half_body(layer, strip, core, local, got_a, got_b, far, start, early, out, total, rounded):
    strength = jnp.log(jnp.float32(LAMBDA / (layer + 1.0)) + 1.0)
    add_up(strip, local, got_a, got_b, far, start, total, rounded)
    parts, _, wide = early.shape
    piece = wide // EARLY
    half = parts * piece
    low_half = core[0] == 0
    for part in range(parts):
        low = part * piece
        mixing = dot(rounded[...], early[part, :, layer * piece : (layer + 1) * piece])
        support = jnp.where(
            low_half, total[:, low : low + piece], total[:, half + low : half + low + piece]
        )
        fresh = jax.nn.relu((1.0 - strength) * support + strength * mixing)
        out[:, low : low + piece] = fresh.astype(BF)


def half_finish(layer, core, local, got_a, got_b, far, start, early):
    rows, width = start.shape
    return pl.pallas_call(
        lambda *refs: half_body(layer, min(256, width), *refs),
        out_shape=pltpu.VMEM((rows, width // 2), BF),
        in_specs=[SM] + [VM] * 6,
        out_specs=VM,
        scratch_shapes=[pltpu.VMEM((rows, width), F32), pltpu.VMEM((rows, width), BF)],
        compiler_params=pltpu.CompilerParams(vmem_limit_bytes=10 << 20),
        name="half_finish",
    )(core, *in_vmem(local, got_a, got_b, far, start, early))


def join_body(core, mine, theirs, picks, new, out_a, out_b):
    half = mine.shape[1]
    edges = out_a.shape[0]

    @pl.when(core[0] == 0)
    def _():
        new[:, :half] = mine[...]
        new[:, half:] = theirs[...]

    @pl.when(core[0] != 0)
    def _():
        new[:, :half] = theirs[...]
        new[:, half:] = mine[...]

    sent = dot(picks[...], new[...]).astype(BF)
    out_a[...] = sent[:edges]
    out_b[...] = sent[edges:]


def join(core, mine, theirs, picks):
    rows, half = mine.shape
    edges = picks.shape[0] // 2
    return pl.pallas_call(
        join_body,
        out_shape=(
            pltpu.VMEM((rows, 2 * half), BF),
            pltpu.VMEM((edges, 2 * half), BF),
            pltpu.VMEM((edges, 2 * half), BF),
        ),
        in_specs=[SM] + [VM] * 3,
        out_specs=(VM, VM, VM),
        compiler_params=pltpu.CompilerParams(vmem_limit_bytes=4 << 20),
        name="join",
    )(core, *in_vmem(mine, theirs, picks))


def finish_body(layer, slot, strip, prefetched, *refs):
    if prefetched:
        local, got_a, got_b, far, picks, start, weight, new, out_a, out_b, total, rounded = refs
    else:
        local, got_a, got_b, far, picks, start, stored = refs[:7]
        new, out_a, out_b, total, rounded, weight, sems = refs[7:]
        copies = []
        for low in range(0, start.shape[1], strip):
            cols = slice(low, low + strip)
            copy = pltpu.make_async_copy(
                stored.at[slot, :, cols], weight.at[:, cols], sems.at[low // strip]
            )
            copy.start()
            copies.append(copy)
    width = start.shape[1]
    edges = got_a.shape[0]
    strength = jnp.log(jnp.float32(LAMBDA / (layer + 1.0)) + 1.0)
    add_up(strip, local, got_a, got_b, far, start, total, rounded)
    for low in range(0, width, strip):
        cols = slice(low, low + strip)
        if not prefetched:
            copies[low // strip].wait()
        mixing = dot(rounded[...], weight[:, cols])
        fresh = jax.nn.relu((1.0 - strength) * total[:, cols] + strength * mixing).astype(BF)
        new[:, cols] = fresh
        sent = dot(picks[...], fresh).astype(BF)
        out_a[:, cols] = sent[:edges]
        out_b[:, cols] = sent[edges:]


def finish(layer, local, got_a, got_b, far, picks, start, weight, prefetched):
    rows, width = start.shape
    edges = got_a.shape[0]
    ins = in_vmem(local, got_a, got_b, far, picks, start)
    scratch = [pltpu.VMEM((rows, width), F32), pltpu.VMEM((rows, width), BF)]
    if prefetched:
        ins += in_vmem(weight)
    else:
        ins.append(pltpu.with_memory_space_constraint(weight, pltpu.HBM))
        scratch += [pltpu.VMEM(weight.shape[1:], BF)]
        scratch += [pltpu.SemaphoreType.DMA((width // min(256, width),))]
    return pl.pallas_call(
        lambda *refs: finish_body(layer, layer - EARLY, min(256, width), prefetched, *refs),
        out_shape=(
            pltpu.VMEM((rows, width), BF),
            pltpu.VMEM((edges, width), BF),
            pltpu.VMEM((edges, width), BF),
        ),
        in_specs=[VM] * 6 + [VM if prefetched else HB],
        out_specs=(VM, VM, VM),
        scratch_shapes=scratch,
        compiler_params=pltpu.CompilerParams(vmem_limit_bytes=10 << 20),
        name="finish",
    )(*ins)


def begin_body(layer, strip, *refs):
    if layer is None:
        current, near, hist, looked, local = refs
    else:
        current, near, hist, looked, stored, local, weight, sem = refs
        copy = pltpu.make_async_copy(stored.at[layer], weight, sem)
        copy.start()
    for low in range(0, current.shape[1], strip):
        cols = slice(low, low + strip)
        local[:, cols] = dot(near[...], current[:, cols]) + dot(hist[...], looked[:, cols])
    if layer is not None:
        copy.wait()


def begin(layer, current, near, hist, looked, stored):
    rows, width = current.shape
    ins = in_vmem(current, near, hist, looked)
    outs = [pltpu.VMEM((rows, width), F32)]
    scratch = []
    if layer is not None:
        ins.append(pltpu.with_memory_space_constraint(stored, pltpu.HBM))
        outs.append(pltpu.VMEM(stored.shape[1:], BF))
        scratch.append(pltpu.SemaphoreType.DMA)
    return pl.pallas_call(
        lambda *refs: begin_body(layer, min(256, width), *refs),
        out_shape=tuple(outs),
        in_specs=[VM] * 4 + [HB] * (layer is not None),
        out_specs=(VM,) * len(outs),
        scratch_shapes=scratch,
        compiler_params=pltpu.CompilerParams(vmem_limit_bytes=4 << 20),
        name="begin",
    )(*ins)


def shards(features, weights, history, own_adj, side_adj, hist_adj, send_ids, hist_ids):
    segment_pos = lax.axis_index("segment")
    segment_count = lax.axis_size("segment")
    graph_count = lax.axis_size("graph")
    core = lax.axis_index("graph") % 2
    chip_odd = (lax.axis_index("graph") // 2) % 2
    layers, _, width = weights.shape
    rows = own_adj.shape[2]
    edge = send_ids.shape[2]
    kept = layers // segment_count
    resident = lax.all_gather(weights[EARLY:], "graph", axis=1, tiled=True)

    piece = width // (2 * segment_count)
    wrows = weights.shape[1]
    columns = weights[:EARLY].reshape(EARLY, wrows, 2, segment_count, piece)
    quarter = lax.dynamic_index_in_dim(columns, segment_pos, 3, keepdims=False)
    quarter = quarter.transpose(2, 1, 0, 3).reshape(1, 2, wrows, EARLY * piece)
    spread = jnp.broadcast_to(quarter, (graph_count // 2, 2, wrows, EARLY * piece))
    spread = spread.reshape(graph_count, wrows, EARLY * piece)
    quarter = lax.all_to_all(spread, "graph", 0, 0, tiled=True).reshape(1, width, EARLY * piece)
    spread = jnp.broadcast_to(quarter, (segment_count, width, EARLY * piece))
    early = lax.all_to_all(spread, "segment", 0, 0, tiled=True)

    def partner(value):
        return lax.ppermute(value, "graph", [(p, p ^ 1) for p in range(graph_count)])

    def exchange(value, first):
        pairs = []
        for p in range(first, graph_count - first - 2, 4):
            for c in range(2):
                pairs += [(p + c, p + c + 2), (p + c + 2, p + c)]
        return lax.ppermute(value, "graph", pairs)

    def pick_batch(value):
        return lax.dynamic_index_in_dim(value, segment_pos, 0, keepdims=False)

    def by_part(mine, theirs):
        return jnp.where(core == 0, mine, theirs), jnp.where(core == 0, theirs, mine)

    initial = lax.dynamic_slice_in_dim(features, segment_pos * rows, rows, 0)
    own = pick_batch(own_adj)
    side = pick_batch(side_adj).reshape(4 * edge, rows)
    hist = pick_batch(hist_adj)
    sids = pick_batch(send_ids).reshape(-1)
    hids = pick_batch(hist_ids)
    tables = jnp.concatenate([own, side, hist], axis=0)
    ids = jnp.concatenate([sids, hids])
    i0, i1 = by_part(ids, partner(ids))
    t0, t1 = by_part(tables, partner(tables))
    x0, x1 = by_part(initial, partner(initial))

    looked = jax.vmap(lambda t: dot(one_hot(hids, t.shape[0]), t).astype(BF))(history)
    g0, g1 = by_part(looked, partner(looked))

    def split(t, i):
        own = t[:rows]
        side = [t[rows + k * edge : rows + (k + 1) * edge] for k in range(4)]
        hist = t[rows + 4 * edge :]
        send = [one_hot(i[k * edge : (k + 1) * edge], rows) for k in range(4)]
        return own, side, hist, send

    own0, side0, hist0, send0 = split(t0, i0)
    own1, side1, hist1, send1 = split(t1, i1)
    q10 = dot_t(side1[0], send0[0]).astype(BF)
    q01 = dot_t(side0[1], send1[1]).astype(BF)
    near = jnp.concatenate(
        [jnp.concatenate([own0, q01], axis=1), jnp.concatenate([q10, own1], axis=1)], axis=0
    )
    zs = jnp.zeros_like(side0[0])
    from_before = jnp.concatenate(
        [
            jnp.concatenate([side0[0], side0[2], zs], axis=0),
            jnp.concatenate([zs, zs, side1[2]], axis=0),
        ],
        axis=1,
    )
    from_after = jnp.concatenate(
        [
            jnp.concatenate([side0[3], zs, zs], axis=0),
            jnp.concatenate([zs, side1[1], side1[3]], axis=0),
        ],
        axis=1,
    )
    to_after = jnp.concatenate(
        [
            jnp.concatenate([zs, send1[0]], axis=1),
            jnp.concatenate([send0[2], zs], axis=1),
            jnp.concatenate([zs, send1[2]], axis=1),
        ],
        axis=0,
    )
    to_before = jnp.concatenate(
        [
            jnp.concatenate([send0[3], zs], axis=1),
            jnp.concatenate([send0[1], zs], axis=1),
            jnp.concatenate([zs, send1[3]], axis=1),
        ],
        axis=0,
    )
    far_a = jnp.where(chip_odd == 0, from_after, from_before)
    far_b = jnp.where(chip_odd == 0, from_before, from_after)
    pick_a = jnp.where(chip_odd == 0, to_after, to_before)
    pick_b = jnp.where(chip_odd == 0, to_before, to_after)
    zh = jnp.zeros_like(hist0)
    hist_t = jnp.concatenate(
        [jnp.concatenate([hist0, zh], axis=1), jnp.concatenate([zh, hist1], axis=1)], axis=0
    )
    looked = jnp.concatenate([g0, g1], axis=1)
    start = jnp.concatenate([x0, x1], axis=0)

    far = jnp.concatenate([far_a, far_b], axis=0).T
    picks = jnp.concatenate([pick_a, pick_b], axis=0)
    hist_n = hist_t.T
    current = start
    sent = dot(picks, current).astype(BF)
    send_a, send_b = sent[: 3 * edge], sent[3 * edge :]
    (local,) = begin(None, current, near, hist_n, looked[0], None)
    place = core.astype(jnp.int32).reshape(1)
    weight = resident
    own_rows = []
    for layer in range(layers):
        got_b = exchange(send_b, 2)
        got_a = exchange(send_a, 0)
        if layer < EARLY:
            mine = half_finish(layer, place, local, got_a, got_b, far, start, early)
            current, send_a, send_b = join(place, mine, partner(mine), picks)
        else:
            current, send_a, send_b = finish(
                layer, local, got_a, got_b, far, picks, start, weight, layer > EARLY
            )
        if layer + 1 < layers:
            brought = layer + 1 - EARLY if layer >= EARLY else None
            out = begin(brought, current, near, hist_n, looked[layer + 1], resident)
            local, weight = (out[0], resident) if brought is None else out
        own_rows.append(lax.dynamic_slice_in_dim(current, core * rows, rows, 0))
    whole = jnp.stack(own_rows)
    return lax.all_to_all(whole, "segment", 0, 1, tiled=True)


def solution(mesh):
    in_specs = (
        P("graph", None),
        P(None, "graph", None),
        P(None, "graph", None),
        P(None, "graph", None),
        P(None, None, "graph", None),
        P(None, "graph", None),
        P(None, None, "graph"),
        P(None, "graph"),
    )
    out_specs = P("segment", "graph", None)
    return jax.shard_map(shards, mesh=mesh, in_specs=in_specs, out_specs=out_specs, check_vma=False)
```

```python
import jax
import jax.numpy as jnp
from jax import lax
from jax.experimental import pallas as pl
from jax.experimental.pallas import tpu as pltpu
from jax.sharding import PartitionSpec as P

ALPHA = 0.1
LAMBDA = 1.5
BF = jnp.bfloat16
F32 = jnp.float32


def dot(a, b):
    return jnp.dot(a, b, preferred_element_type=F32)


def dot_t(a, b):
    return lax.dot_general(a, b, (((0,), (0,)), ((), ())), preferred_element_type=F32)


def one_hot(ids, width):
    return (ids[:, None] == lax.broadcasted_iota(jnp.int32, (ids.shape[0], width), 1)).astype(BF)


VM = pl.BlockSpec(memory_space=pltpu.VMEM)
HB = pl.BlockSpec(memory_space=pltpu.HBM)
SM = pl.BlockSpec(memory_space=pltpu.SMEM)
EARLY = 2


def in_vmem(*values):
    return [pltpu.with_memory_space_constraint(v, pltpu.VMEM) for v in values]


def add_up(strip, local, got_a, got_b, far, start, total, rounded):
    for low in range(0, start.shape[1], strip):
        cols = slice(low, low + strip)
        got = jnp.concatenate([got_a[:, cols], got_b[:, cols]], axis=0)
        summed = local[:, cols] + dot(far[...], got)
        support = (1.0 - ALPHA) * summed + ALPHA * start[:, cols].astype(F32)
        total[:, cols] = support
        rounded[:, cols] = support.astype(BF)


def half_body(layer, strip, core, local, got_a, got_b, far, start, early, out, total, rounded):
    strength = jnp.log(jnp.float32(LAMBDA / (layer + 1.0)) + 1.0)
    add_up(strip, local, got_a, got_b, far, start, total, rounded)
    parts, _, piece = early.shape
    half = parts * piece
    low_half = core[0] == 0
    for part in range(parts):
        low = part * piece
        mixing = dot(rounded[...], early[part])
        support = jnp.where(
            low_half, total[:, low : low + piece], total[:, half + low : half + low + piece]
        )
        fresh = jax.nn.relu((1.0 - strength) * support + strength * mixing)
        out[:, low : low + piece] = fresh.astype(BF)


def half_finish(layer, core, local, got_a, got_b, far, start, early):
    rows, width = start.shape
    return pl.pallas_call(
        lambda *refs: half_body(layer, min(256, width), *refs),
        out_shape=pltpu.VMEM((rows, width // 2), BF),
        in_specs=[SM] + [VM] * 6,
        out_specs=VM,
        scratch_shapes=[pltpu.VMEM((rows, width), F32), pltpu.VMEM((rows, width), BF)],
        compiler_params=pltpu.CompilerParams(vmem_limit_bytes=10 << 20),
        name="half_finish",
    )(core, *in_vmem(local, got_a, got_b, far, start, early))


def join_body(core, mine, theirs, picks, new, out_a, out_b):
    half = mine.shape[1]
    edges = out_a.shape[0]

    @pl.when(core[0] == 0)
    def _():
        new[:, :half] = mine[...]
        new[:, half:] = theirs[...]

    @pl.when(core[0] != 0)
    def _():
        new[:, :half] = theirs[...]
        new[:, half:] = mine[...]

    sent = dot(picks[...], new[...]).astype(BF)
    out_a[...] = sent[:edges]
    out_b[...] = sent[edges:]


def join(core, mine, theirs, picks):
    rows, half = mine.shape
    edges = picks.shape[0] // 2
    return pl.pallas_call(
        join_body,
        out_shape=(
            pltpu.VMEM((rows, 2 * half), BF),
            pltpu.VMEM((edges, 2 * half), BF),
            pltpu.VMEM((edges, 2 * half), BF),
        ),
        in_specs=[SM] + [VM] * 3,
        out_specs=(VM, VM, VM),
        compiler_params=pltpu.CompilerParams(vmem_limit_bytes=4 << 20),
        name="join",
    )(core, *in_vmem(mine, theirs, picks))


def finish_body(layer, strip, *refs):
    local, got_a, got_b, far, picks, start, weight, new, out_a, out_b, total, rounded = refs
    edges = got_a.shape[0]
    strength = jnp.log(jnp.float32(LAMBDA / (layer + 1.0)) + 1.0)
    add_up(strip, local, got_a, got_b, far, start, total, rounded)
    for low in range(0, start.shape[1], strip):
        cols = slice(low, low + strip)
        mixing = dot(rounded[...], weight[:, cols])
        fresh = jax.nn.relu((1.0 - strength) * total[:, cols] + strength * mixing).astype(BF)
        new[:, cols] = fresh
        sent = dot(picks[...], fresh).astype(BF)
        out_a[:, cols] = sent[:edges]
        out_b[:, cols] = sent[edges:]


def finish(layer, local, got_a, got_b, far, picks, start, weight):
    rows, width = start.shape
    edges = got_a.shape[0]
    return pl.pallas_call(
        lambda *refs: finish_body(layer, min(256, width), *refs),
        out_shape=(
            pltpu.VMEM((rows, width), BF),
            pltpu.VMEM((edges, width), BF),
            pltpu.VMEM((edges, width), BF),
        ),
        in_specs=[VM] * 7,
        out_specs=(VM, VM, VM),
        scratch_shapes=[pltpu.VMEM((rows, width), F32), pltpu.VMEM((rows, width), BF)],
        compiler_params=pltpu.CompilerParams(vmem_limit_bytes=6 << 20),
        name="finish",
    )(*in_vmem(local, got_a, got_b, far, picks, start, weight))


def begin_body(layer, strip, *refs):
    if layer is None:
        current, near, hist, looked, local = refs
    else:
        current, near, hist, looked, stored, local, weight, sem = refs
        copy = pltpu.make_async_copy(stored.at[layer], weight, sem)
        copy.start()
    for low in range(0, current.shape[1], strip):
        cols = slice(low, low + strip)
        local[:, cols] = dot(near[...], current[:, cols]) + dot(hist[...], looked[:, cols])
    if layer is not None:
        copy.wait()


def begin(layer, current, near, hist, looked, stored):
    rows, width = current.shape
    ins = in_vmem(current, near, hist, looked)
    outs = [pltpu.VMEM((rows, width), F32)]
    scratch = []
    if layer is not None:
        ins.append(pltpu.with_memory_space_constraint(stored, pltpu.HBM))
        outs.append(pltpu.VMEM(stored.shape[1:], BF))
        scratch.append(pltpu.SemaphoreType.DMA)
    return pl.pallas_call(
        lambda *refs: begin_body(layer, min(256, width), *refs),
        out_shape=tuple(outs),
        in_specs=[VM] * 4 + [HB] * (layer is not None),
        out_specs=(VM,) * len(outs),
        scratch_shapes=scratch,
        compiler_params=pltpu.CompilerParams(vmem_limit_bytes=4 << 20),
        name="begin",
    )(*ins)


def shards(features, weights, history, own_adj, side_adj, hist_adj, send_ids, hist_ids):
    segment_pos = lax.axis_index("segment")
    segment_count = lax.axis_size("segment")
    graph_count = lax.axis_size("graph")
    core = lax.axis_index("graph") % 2
    chip_odd = (lax.axis_index("graph") // 2) % 2
    layers, _, width = weights.shape
    rows = own_adj.shape[2]
    edge = send_ids.shape[2]
    resident = lax.all_gather(weights[EARLY:], "graph", axis=1, tiled=True)

    piece = width // (2 * segment_count)
    wrows = weights.shape[1]
    columns = weights[:EARLY].reshape(EARLY, wrows, 2, segment_count, piece)
    quarter = lax.dynamic_index_in_dim(columns, segment_pos, 3, keepdims=False)
    quarter = quarter.transpose(2, 1, 0, 3).reshape(1, 2, wrows, EARLY * piece)
    spread = jnp.broadcast_to(quarter, (graph_count // 2, 2, wrows, EARLY * piece))
    spread = spread.reshape(graph_count, wrows, EARLY * piece)
    quarter = lax.all_to_all(spread, "graph", 0, 0, tiled=True).reshape(1, width, EARLY * piece)

    def early_weight(layer, after):
        part = quarter[:, :, layer * piece : (layer + 1) * piece]
        part = jnp.broadcast_to(part, (segment_count, width, piece))
        if after is not None:
            part, after = lax.optimization_barrier((part, after))
        return lax.all_to_all(part, "segment", 0, 0, tiled=True), after

    def swap(value):
        return lax.ppermute(value, "graph", [(p, p ^ 1) for p in range(graph_count)])

    def exchange(value, first):
        pairs = []
        for p in range(first, graph_count - first - 2, 4):
            for c in range(2):
                pairs += [(p + c, p + c + 2), (p + c + 2, p + c)]
        return lax.ppermute(value, "graph", pairs)

    def pick_batch(value):
        return lax.dynamic_index_in_dim(value, segment_pos, 0, keepdims=False)

    def by_part(mine, theirs):
        return jnp.where(core == 0, mine, theirs), jnp.where(core == 0, theirs, mine)

    initial = lax.dynamic_slice_in_dim(features, segment_pos * rows, rows, 0)
    own = pick_batch(own_adj)
    side = pick_batch(side_adj).reshape(4 * edge, rows)
    hist = pick_batch(hist_adj)
    sids = pick_batch(send_ids).reshape(-1)
    hids = pick_batch(hist_ids)
    tables = jnp.concatenate([own, side, hist], axis=0)
    ids = jnp.concatenate([sids, hids])
    i0, i1 = by_part(ids, swap(ids))
    t0, t1 = by_part(tables, swap(tables))
    x0, x1 = by_part(initial, swap(initial))

    looked = jax.vmap(lambda t: dot(one_hot(hids, t.shape[0]), t).astype(BF))(history)
    g0, g1 = by_part(looked, swap(looked))

    def split(t, i):
        own = t[:rows]
        side = [t[rows + k * edge : rows + (k + 1) * edge] for k in range(4)]
        hist = t[rows + 4 * edge :]
        send = [one_hot(i[k * edge : (k + 1) * edge], rows) for k in range(4)]
        return own, side, hist, send

    own0, side0, hist0, send0 = split(t0, i0)
    own1, side1, hist1, send1 = split(t1, i1)
    q10 = dot_t(side1[0], send0[0]).astype(BF)
    q01 = dot_t(side0[1], send1[1]).astype(BF)
    near = jnp.concatenate(
        [jnp.concatenate([own0, q01], axis=1), jnp.concatenate([q10, own1], axis=1)], axis=0
    )
    zs = jnp.zeros_like(side0[0])
    from_before = jnp.concatenate(
        [
            jnp.concatenate([side0[0], side0[2], zs], axis=0),
            jnp.concatenate([zs, zs, side1[2]], axis=0),
        ],
        axis=1,
    )
    from_after = jnp.concatenate(
        [
            jnp.concatenate([side0[3], zs, zs], axis=0),
            jnp.concatenate([zs, side1[1], side1[3]], axis=0),
        ],
        axis=1,
    )
    to_after = jnp.concatenate(
        [
            jnp.concatenate([zs, send1[0]], axis=1),
            jnp.concatenate([send0[2], zs], axis=1),
            jnp.concatenate([zs, send1[2]], axis=1),
        ],
        axis=0,
    )
    to_before = jnp.concatenate(
        [
            jnp.concatenate([send0[3], zs], axis=1),
            jnp.concatenate([send0[1], zs], axis=1),
            jnp.concatenate([zs, send1[3]], axis=1),
        ],
        axis=0,
    )
    far_a = jnp.where(chip_odd == 0, from_after, from_before)
    far_b = jnp.where(chip_odd == 0, from_before, from_after)
    pick_a = jnp.where(chip_odd == 0, to_after, to_before)
    pick_b = jnp.where(chip_odd == 0, to_before, to_after)
    zh = jnp.zeros_like(hist0)
    hist_t = jnp.concatenate(
        [jnp.concatenate([hist0, zh], axis=1), jnp.concatenate([zh, hist1], axis=1)], axis=0
    )
    looked = jnp.concatenate([g0, g1], axis=1)
    start = jnp.concatenate([x0, x1], axis=0)

    far = jnp.concatenate([far_a, far_b], axis=0).T
    picks = jnp.concatenate([pick_a, pick_b], axis=0)
    hist_n = hist_t.T
    current = start
    sent = dot(picks, current).astype(BF)
    send_a, send_b = sent[: 3 * edge], sent[3 * edge :]
    (local,) = begin(None, current, near, hist_n, looked[0], None)
    place = core.astype(jnp.int32).reshape(1)
    early, _ = early_weight(0, None)
    weight = None
    own_rows = []
    for layer in range(layers):
        got_b = exchange(send_b, 2)
        got_a = exchange(send_a, 0)
        if layer < EARLY:
            mine = half_finish(layer, place, local, got_a, got_b, far, start, early)
            if layer + 1 < EARLY:
                early, mine = early_weight(layer + 1, mine)
            current, send_a, send_b = join(place, mine, swap(mine), picks)
        else:
            current, send_a, send_b = finish(
                layer, local, got_a, got_b, far, picks, start, weight
            )
        if layer + 1 < layers:
            brought = layer + 1 - EARLY if layer + 1 >= EARLY else None
            out = begin(brought, current, near, hist_n, looked[layer + 1], resident)
            local, weight = (out[0], None) if brought is None else out
        own_rows.append(lax.dynamic_slice_in_dim(current, core * rows, rows, 0))
    whole = jnp.stack(own_rows)
    return lax.all_to_all(whole, "segment", 0, 1, tiled=True)


def solution(mesh):
    in_specs = (
        P("graph", None),
        P(None, "graph", None),
        P(None, "graph", None),
        P(None, "graph", None),
        P(None, None, "graph", None),
        P(None, "graph", None),
        P(None, None, "graph"),
        P(None, "graph"),
    )
    out_specs = P("segment", "graph", None)
    return jax.shard_map(shards, mesh=mesh, in_specs=in_specs, out_specs=out_specs, check_vma=False)
```

```python
import jax
import jax.numpy as jnp
from jax import lax
from jax.experimental import pallas as pl
from jax.experimental.pallas import tpu as pltpu
from jax.sharding import PartitionSpec as P

ALPHA = 0.1
LAMBDA = 1.5
BF = jnp.bfloat16
F32 = jnp.float32


def dot(a, b):
    return jnp.dot(a, b, preferred_element_type=F32)


def dot_t(a, b):
    return lax.dot_general(a, b, (((0,), (0,)), ((), ())), preferred_element_type=F32)


def one_hot(ids, width):
    return (ids[:, None] == lax.broadcasted_iota(jnp.int32, (ids.shape[0], width), 1)).astype(BF)


VM = pl.BlockSpec(memory_space=pltpu.VMEM)
HB = pl.BlockSpec(memory_space=pltpu.HBM)
SM = pl.BlockSpec(memory_space=pltpu.SMEM)
EARLY = 2


def in_vmem(*values):
    return [pltpu.with_memory_space_constraint(v, pltpu.VMEM) for v in values]


def add_up(strip, local, got_a, got_b, far, start, total, rounded):
    for low in range(0, start.shape[1], strip):
        cols = slice(low, low + strip)
        got = jnp.concatenate([got_a[:, cols], got_b[:, cols]], axis=0)
        summed = local[:, cols] + dot(far[...], got)
        support = (1.0 - ALPHA) * summed + ALPHA * start[:, cols].astype(F32)
        total[:, cols] = support
        rounded[:, cols] = support.astype(BF)


def half_body(layer, strip, core, local, got_a, got_b, far, start, early, out, total, rounded):
    strength = jnp.log(jnp.float32(LAMBDA / (layer + 1.0)) + 1.0)
    add_up(strip, local, got_a, got_b, far, start, total, rounded)
    parts, _, piece = early.shape
    half = parts * piece
    low_half = core[0] == 0
    for part in range(parts):
        low = part * piece
        mixing = dot(rounded[...], early[part])
        support = jnp.where(
            low_half, total[:, low : low + piece], total[:, half + low : half + low + piece]
        )
        fresh = jax.nn.relu((1.0 - strength) * support + strength * mixing)
        out[:, low : low + piece] = fresh.astype(BF)


def half_finish(layer, core, local, got_a, got_b, far, start, early):
    rows, width = start.shape
    return pl.pallas_call(
        lambda *refs: half_body(layer, min(256, width), *refs),
        out_shape=pltpu.VMEM((rows, width // 2), BF),
        in_specs=[SM] + [VM] * 6,
        out_specs=VM,
        scratch_shapes=[pltpu.VMEM((rows, width), F32), pltpu.VMEM((rows, width), BF)],
        compiler_params=pltpu.CompilerParams(vmem_limit_bytes=10 << 20),
        name="half_finish",
    )(core, *in_vmem(local, got_a, got_b, far, start, early))


def join_body(core, mine, theirs, picks, new, out_a, out_b):
    half = mine.shape[1]
    edges = out_a.shape[0]

    @pl.when(core[0] == 0)
    def _():
        new[:, :half] = mine[...]
        new[:, half:] = theirs[...]

    @pl.when(core[0] != 0)
    def _():
        new[:, :half] = theirs[...]
        new[:, half:] = mine[...]

    sent = dot(picks[...], new[...]).astype(BF)
    out_a[...] = sent[:edges]
    out_b[...] = sent[edges:]


def join(core, mine, theirs, picks):
    rows, half = mine.shape
    edges = picks.shape[0] // 2
    return pl.pallas_call(
        join_body,
        out_shape=(
            pltpu.VMEM((rows, 2 * half), BF),
            pltpu.VMEM((edges, 2 * half), BF),
            pltpu.VMEM((edges, 2 * half), BF),
        ),
        in_specs=[SM] + [VM] * 3,
        out_specs=(VM, VM, VM),
        compiler_params=pltpu.CompilerParams(vmem_limit_bytes=4 << 20),
        name="join",
    )(core, *in_vmem(mine, theirs, picks))


def finish_body(layer, strip, *refs):
    local, got_a, got_b, far, picks, start, weight, new, out_a, out_b, total, rounded = refs
    edges = got_a.shape[0]
    strength = jnp.log(jnp.float32(LAMBDA / (layer + 1.0)) + 1.0)
    add_up(strip, local, got_a, got_b, far, start, total, rounded)
    for low in range(0, start.shape[1], strip):
        cols = slice(low, low + strip)
        mixing = dot(rounded[...], weight[:, cols])
        fresh = jax.nn.relu((1.0 - strength) * total[:, cols] + strength * mixing).astype(BF)
        new[:, cols] = fresh
        sent = dot(picks[...], fresh).astype(BF)
        out_a[:, cols] = sent[:edges]
        out_b[:, cols] = sent[edges:]


def finish(layer, local, got_a, got_b, far, picks, start, weight):
    rows, width = start.shape
    edges = got_a.shape[0]
    return pl.pallas_call(
        lambda *refs: finish_body(layer, min(256, width), *refs),
        out_shape=(
            pltpu.VMEM((rows, width), BF),
            pltpu.VMEM((edges, width), BF),
            pltpu.VMEM((edges, width), BF),
        ),
        in_specs=[VM] * 7,
        out_specs=(VM, VM, VM),
        scratch_shapes=[pltpu.VMEM((rows, width), F32), pltpu.VMEM((rows, width), BF)],
        compiler_params=pltpu.CompilerParams(vmem_limit_bytes=6 << 20),
        name="finish",
    )(*in_vmem(local, got_a, got_b, far, picks, start, weight))


def begin_body(layer, strip, *refs):
    if layer is None:
        current, near, hist, looked, local = refs
    else:
        current, near, hist, looked, stored, local, weight, sem = refs
        copy = pltpu.make_async_copy(stored.at[layer], weight, sem)
        copy.start()
    for low in range(0, current.shape[1], strip):
        cols = slice(low, low + strip)
        local[:, cols] = dot(near[...], current[:, cols]) + dot(hist[...], looked[:, cols])
    if layer is not None:
        copy.wait()


def begin(layer, current, near, hist, looked, stored):
    rows, width = current.shape
    ins = in_vmem(current, near, hist, looked)
    outs = [pltpu.VMEM((rows, width), F32)]
    scratch = []
    if layer is not None:
        ins.append(pltpu.with_memory_space_constraint(stored, pltpu.HBM))
        outs.append(pltpu.VMEM(stored.shape[1:], BF))
        scratch.append(pltpu.SemaphoreType.DMA)
    return pl.pallas_call(
        lambda *refs: begin_body(layer, min(256, width), *refs),
        out_shape=tuple(outs),
        in_specs=[VM] * 4 + [HB] * (layer is not None),
        out_specs=(VM,) * len(outs),
        scratch_shapes=scratch,
        compiler_params=pltpu.CompilerParams(vmem_limit_bytes=4 << 20),
        name="begin",
    )(*ins)


def shards(features, weights, history, own_adj, side_adj, hist_adj, send_ids, hist_ids):
    segment_pos = lax.axis_index("segment")
    segment_count = lax.axis_size("segment")
    graph_count = lax.axis_size("graph")
    core = lax.axis_index("graph") % 2
    chip_odd = (lax.axis_index("graph") // 2) % 2
    layers, _, width = weights.shape
    rows = own_adj.shape[2]
    edge = send_ids.shape[2]
    resident = lax.all_gather(weights[EARLY:], "graph", axis=1, tiled=True)

    piece = width // (2 * segment_count)
    wrows = weights.shape[1]
    columns = weights[:EARLY].reshape(EARLY, wrows, 2, segment_count, piece)
    quarter = lax.dynamic_index_in_dim(columns, segment_pos, 3, keepdims=False)
    quarter = quarter.transpose(2, 1, 0, 3).reshape(1, 2, wrows, EARLY * piece)
    spread = jnp.broadcast_to(quarter, (graph_count // 2, 2, wrows, EARLY * piece))
    spread = spread.reshape(graph_count, wrows, EARLY * piece)
    quarter = lax.all_to_all(spread, "graph", 0, 0, tiled=True).reshape(1, width, EARLY * piece)

    def early_weight(layer, after):
        part = quarter[:, :, layer * piece : (layer + 1) * piece]
        part = jnp.broadcast_to(part, (segment_count, width, piece))
        if after is not None:
            part, after = lax.optimization_barrier((part, after))
        return lax.all_to_all(part, "segment", 0, 0, tiled=True), after

    def swap(value):
        return lax.ppermute(value, "graph", [(p, p ^ 1) for p in range(graph_count)])

    def exchange(value, first):
        pairs = []
        for p in range(first, graph_count - first - 2, 4):
            for c in range(2):
                pairs += [(p + c, p + c + 2), (p + c + 2, p + c)]
        return lax.ppermute(value, "graph", pairs)

    def pick_batch(value):
        return lax.dynamic_index_in_dim(value, segment_pos, 0, keepdims=False)

    def by_part(mine, theirs):
        return jnp.where(core == 0, mine, theirs), jnp.where(core == 0, theirs, mine)

    initial = lax.dynamic_slice_in_dim(features, segment_pos * rows, rows, 0)
    own = pick_batch(own_adj)
    side = pick_batch(side_adj).reshape(4 * edge, rows)
    hist = pick_batch(hist_adj)
    sids = pick_batch(send_ids).reshape(-1)
    hids = pick_batch(hist_ids)
    listed = jnp.pad(sids.astype(BF).reshape(4, edge), ((0, 12), (0, rows - edge)))
    tables = jnp.concatenate([own, side, hist, listed], axis=0)
    t0, t1 = by_part(tables, swap(tables))
    i0, i1 = [
        t[-16:-12, :edge].astype(jnp.int32).reshape(-1) for t in (t0, t1)
    ]
    x0, x1 = by_part(initial, swap(initial))

    looked = jax.vmap(lambda t: dot(one_hot(hids, t.shape[0]), t).astype(BF))(history)
    g0, g1 = by_part(looked, swap(looked))

    def split(t, i):
        own = t[:rows]
        side = [t[rows + k * edge : rows + (k + 1) * edge] for k in range(4)]
        hist = t[rows + 4 * edge : -16]
        send = [one_hot(i[k * edge : (k + 1) * edge], rows) for k in range(4)]
        return own, side, hist, send

    own0, side0, hist0, send0 = split(t0, i0)
    own1, side1, hist1, send1 = split(t1, i1)
    q10 = dot_t(side1[0], send0[0]).astype(BF)
    q01 = dot_t(side0[1], send1[1]).astype(BF)
    near = jnp.concatenate(
        [jnp.concatenate([own0, q01], axis=1), jnp.concatenate([q10, own1], axis=1)], axis=0
    )
    zs = jnp.zeros_like(side0[0])
    from_before = jnp.concatenate(
        [
            jnp.concatenate([side0[0], side0[2], zs], axis=0),
            jnp.concatenate([zs, zs, side1[2]], axis=0),
        ],
        axis=1,
    )
    from_after = jnp.concatenate(
        [
            jnp.concatenate([side0[3], zs, zs], axis=0),
            jnp.concatenate([zs, side1[1], side1[3]], axis=0),
        ],
        axis=1,
    )
    to_after = jnp.concatenate(
        [
            jnp.concatenate([zs, send1[0]], axis=1),
            jnp.concatenate([send0[2], zs], axis=1),
            jnp.concatenate([zs, send1[2]], axis=1),
        ],
        axis=0,
    )
    to_before = jnp.concatenate(
        [
            jnp.concatenate([send0[3], zs], axis=1),
            jnp.concatenate([send0[1], zs], axis=1),
            jnp.concatenate([zs, send1[3]], axis=1),
        ],
        axis=0,
    )
    far_a = jnp.where(chip_odd == 0, from_after, from_before)
    far_b = jnp.where(chip_odd == 0, from_before, from_after)
    pick_a = jnp.where(chip_odd == 0, to_after, to_before)
    pick_b = jnp.where(chip_odd == 0, to_before, to_after)
    zh = jnp.zeros_like(hist0)
    hist_t = jnp.concatenate(
        [jnp.concatenate([hist0, zh], axis=1), jnp.concatenate([zh, hist1], axis=1)], axis=0
    )
    looked = jnp.concatenate([g0, g1], axis=1)
    start = jnp.concatenate([x0, x1], axis=0)

    far = jnp.concatenate([far_a, far_b], axis=0).T
    picks = jnp.concatenate([pick_a, pick_b], axis=0)
    hist_n = hist_t.T
    current = start
    sent = dot(picks, current).astype(BF)
    send_a, send_b = sent[: 3 * edge], sent[3 * edge :]
    place = core.astype(jnp.int32).reshape(1)
    early = [early_weight(0, None)[0]]
    for layer in range(1, EARLY):
        arriving, early[-1] = early_weight(layer, early[-1])
        early.append(arriving)
    held, early[0] = lax.optimization_barrier((current, early[0]))
    (local,) = begin(None, held, near, hist_n, looked[0], None)
    weight = None
    own_rows = []
    for layer in range(layers):
        got_b = exchange(send_b, 2)
        got_a = exchange(send_a, 0)
        if layer < EARLY:
            mine = half_finish(layer, place, local, got_a, got_b, far, start, early[layer])
            current, send_a, send_b = join(place, mine, swap(mine), picks)
        else:
            current, send_a, send_b = finish(
                layer, local, got_a, got_b, far, picks, start, weight
            )
        if layer + 1 < layers:
            brought = layer + 1 - EARLY if layer + 1 >= EARLY else None
            held = current
            if layer + 1 < EARLY:
                held, early[layer + 1] = lax.optimization_barrier((current, early[layer + 1]))
            out = begin(brought, held, near, hist_n, looked[layer + 1], resident)
            local, weight = (out[0], None) if brought is None else out
        own_rows.append(lax.dynamic_slice_in_dim(current, core * rows, rows, 0))
    whole = jnp.stack(own_rows)
    return lax.all_to_all(whole, "segment", 0, 1, tiled=True)


def solution(mesh):
    in_specs = (
        P("graph", None),
        P(None, "graph", None),
        P(None, "graph", None),
        P(None, "graph", None),
        P(None, None, "graph", None),
        P(None, "graph", None),
        P(None, None, "graph"),
        P(None, "graph"),
    )
    out_specs = P("segment", "graph", None)
    return jax.shard_map(shards, mesh=mesh, in_specs=in_specs, out_specs=out_specs, check_vma=False)
```

```python
import jax
import jax.numpy as jnp
from jax import lax
from jax.experimental import pallas as pl
from jax.experimental.pallas import tpu as pltpu
from jax.sharding import PartitionSpec as P

ALPHA = 0.1
LAMBDA = 1.5
BF = jnp.bfloat16
F32 = jnp.float32


def dot(a, b):
    return jnp.dot(a, b, preferred_element_type=F32)


def dot_t(a, b):
    return lax.dot_general(a, b, (((0,), (0,)), ((), ())), preferred_element_type=F32)


def one_hot(ids, width):
    return (ids[:, None] == lax.broadcasted_iota(jnp.int32, (ids.shape[0], width), 1)).astype(BF)


VM = pl.BlockSpec(memory_space=pltpu.VMEM)
HB = pl.BlockSpec(memory_space=pltpu.HBM)
SM = pl.BlockSpec(memory_space=pltpu.SMEM)
EARLY = 2


def in_vmem(*values):
    return [pltpu.with_memory_space_constraint(v, pltpu.VMEM) for v in values]


def add_up(strip, local, got_a, got_b, far, start, total, rounded):
    for low in range(0, start.shape[1], strip):
        cols = slice(low, low + strip)
        got = jnp.concatenate([got_a[:, cols], got_b[:, cols]], axis=0)
        summed = local[:, cols] + dot(far[...], got)
        support = (1.0 - ALPHA) * summed + ALPHA * start[:, cols].astype(F32)
        total[:, cols] = support
        rounded[:, cols] = support.astype(BF)


def half_body(layer, strip, core, local, got_a, got_b, far, start, early, out, total, rounded):
    strength = jnp.log(jnp.float32(LAMBDA / (layer + 1.0)) + 1.0)
    add_up(strip, local, got_a, got_b, far, start, total, rounded)
    parts, _, piece = early.shape
    half = parts * piece
    low_half = core[0] == 0
    for part in range(parts):
        low = part * piece
        mixing = dot(rounded[...], early[part])
        support = jnp.where(
            low_half, total[:, low : low + piece], total[:, half + low : half + low + piece]
        )
        fresh = jax.nn.relu((1.0 - strength) * support + strength * mixing)
        out[:, low : low + piece] = fresh.astype(BF)


def half_finish(layer, core, local, got_a, got_b, far, start, early):
    rows, width = start.shape
    return pl.pallas_call(
        lambda *refs: half_body(layer, min(512, width), *refs),
        out_shape=pltpu.VMEM((rows, width // 2), BF),
        in_specs=[SM] + [VM] * 6,
        out_specs=VM,
        scratch_shapes=[pltpu.VMEM((rows, width), F32), pltpu.VMEM((rows, width), BF)],
        compiler_params=pltpu.CompilerParams(vmem_limit_bytes=10 << 20),
        name="half_finish",
    )(core, *in_vmem(local, got_a, got_b, far, start, early))


def join_body(core, mine, theirs, picks, new, out_a, out_b):
    half = mine.shape[1]
    edges = out_a.shape[0]

    @pl.when(core[0] == 0)
    def _():
        new[:, :half] = mine[...]
        new[:, half:] = theirs[...]

    @pl.when(core[0] != 0)
    def _():
        new[:, :half] = theirs[...]
        new[:, half:] = mine[...]

    sent = dot(picks[...], new[...]).astype(BF)
    out_a[...] = sent[:edges]
    out_b[...] = sent[edges:]


def join(core, mine, theirs, picks):
    rows, half = mine.shape
    edges = picks.shape[0] // 2
    return pl.pallas_call(
        join_body,
        out_shape=(
            pltpu.VMEM((rows, 2 * half), BF),
            pltpu.VMEM((edges, 2 * half), BF),
            pltpu.VMEM((edges, 2 * half), BF),
        ),
        in_specs=[SM] + [VM] * 3,
        out_specs=(VM, VM, VM),
        compiler_params=pltpu.CompilerParams(vmem_limit_bytes=4 << 20),
        name="join",
    )(core, *in_vmem(mine, theirs, picks))


def finish_body(layer, strip, *refs):
    local, got_a, got_b, far, picks, start, weight, new, out_a, out_b, total, rounded = refs
    edges = got_a.shape[0]
    strength = jnp.log(jnp.float32(LAMBDA / (layer + 1.0)) + 1.0)
    add_up(strip, local, got_a, got_b, far, start, total, rounded)
    for low in range(0, start.shape[1], strip):
        cols = slice(low, low + strip)
        mixing = dot(rounded[...], weight[:, cols])
        fresh = jax.nn.relu((1.0 - strength) * total[:, cols] + strength * mixing).astype(BF)
        new[:, cols] = fresh
        sent = dot(picks[...], fresh).astype(BF)
        out_a[:, cols] = sent[:edges]
        out_b[:, cols] = sent[edges:]


def finish(layer, local, got_a, got_b, far, picks, start, weight):
    rows, width = start.shape
    edges = got_a.shape[0]
    return pl.pallas_call(
        lambda *refs: finish_body(layer, min(512, width), *refs),
        out_shape=(
            pltpu.VMEM((rows, width), BF),
            pltpu.VMEM((edges, width), BF),
            pltpu.VMEM((edges, width), BF),
        ),
        in_specs=[VM] * 7,
        out_specs=(VM, VM, VM),
        scratch_shapes=[pltpu.VMEM((rows, width), F32), pltpu.VMEM((rows, width), BF)],
        compiler_params=pltpu.CompilerParams(vmem_limit_bytes=8 << 20),
        name="finish",
    )(*in_vmem(local, got_a, got_b, far, picks, start, weight))


def begin_body(layer, strip, *refs):
    if layer is None:
        current, near, hist, looked, local = refs
    else:
        current, near, hist, looked, stored, local, weight, sem = refs
        copy = pltpu.make_async_copy(stored.at[layer], weight, sem)
        copy.start()
    for low in range(0, current.shape[1], strip):
        cols = slice(low, low + strip)
        local[:, cols] = dot(near[...], current[:, cols]) + dot(hist[...], looked[:, cols])
    if layer is not None:
        copy.wait()


def begin(layer, current, near, hist, looked, stored):
    rows, width = current.shape
    ins = in_vmem(current, near, hist, looked)
    outs = [pltpu.VMEM((rows, width), F32)]
    scratch = []
    if layer is not None:
        ins.append(pltpu.with_memory_space_constraint(stored, pltpu.HBM))
        outs.append(pltpu.VMEM(stored.shape[1:], BF))
        scratch.append(pltpu.SemaphoreType.DMA)
    return pl.pallas_call(
        lambda *refs: begin_body(layer, min(256, width), *refs),
        out_shape=tuple(outs),
        in_specs=[VM] * 4 + [HB] * (layer is not None),
        out_specs=(VM,) * len(outs),
        scratch_shapes=scratch,
        compiler_params=pltpu.CompilerParams(vmem_limit_bytes=4 << 20),
        name="begin",
    )(*ins)


def shards(features, weights, history, own_adj, side_adj, hist_adj, send_ids, hist_ids):
    segment_pos = lax.axis_index("segment")
    segment_count = lax.axis_size("segment")
    graph_count = lax.axis_size("graph")
    core = lax.axis_index("graph") % 2
    chip_odd = (lax.axis_index("graph") // 2) % 2
    layers, _, width = weights.shape
    rows = own_adj.shape[2]
    edge = send_ids.shape[2]
    resident = lax.all_gather(weights[EARLY:], "graph", axis=1, tiled=True)

    piece = width // (2 * segment_count)
    wrows = weights.shape[1]
    columns = weights[:EARLY].reshape(EARLY, wrows, 2, segment_count, piece)
    quarter = lax.dynamic_index_in_dim(columns, segment_pos, 3, keepdims=False)
    quarter = quarter.transpose(2, 1, 0, 3).reshape(1, 2, wrows, EARLY * piece)
    spread = jnp.broadcast_to(quarter, (graph_count // 2, 2, wrows, EARLY * piece))
    spread = spread.reshape(graph_count, wrows, EARLY * piece)
    quarter = lax.all_to_all(spread, "graph", 0, 0, tiled=True).reshape(1, width, EARLY * piece)

    def early_weight(layer, after):
        part = quarter[:, :, layer * piece : (layer + 1) * piece]
        part = jnp.broadcast_to(part, (segment_count, width, piece))
        if after is not None:
            part, after = lax.optimization_barrier((part, after))
        return lax.all_to_all(part, "segment", 0, 0, tiled=True), after

    def swap(value):
        return lax.ppermute(value, "graph", [(p, p ^ 1) for p in range(graph_count)])

    def exchange(value, first):
        pairs = []
        for p in range(first, graph_count - first - 2, 4):
            for c in range(2):
                pairs += [(p + c, p + c + 2), (p + c + 2, p + c)]
        return lax.ppermute(value, "graph", pairs)

    def pick_batch(value):
        return lax.dynamic_index_in_dim(value, segment_pos, 0, keepdims=False)

    def by_part(mine, theirs):
        return jnp.where(core == 0, mine, theirs), jnp.where(core == 0, theirs, mine)

    initial = lax.dynamic_slice_in_dim(features, segment_pos * rows, rows, 0)
    own = pick_batch(own_adj)
    side = pick_batch(side_adj).reshape(4 * edge, rows)
    hist = pick_batch(hist_adj)
    sids = pick_batch(send_ids).reshape(-1)
    hids = pick_batch(hist_ids)
    listed = jnp.pad(sids.astype(BF).reshape(4, edge), ((0, 12), (0, rows - edge)))
    tables = jnp.concatenate([own, side, hist, listed], axis=0)
    t0, t1 = by_part(tables, swap(tables))
    i0, i1 = [
        t[-16:-12, :edge].astype(jnp.int32).reshape(-1) for t in (t0, t1)
    ]
    x0, x1 = by_part(initial, swap(initial))

    looked = jax.vmap(lambda t: dot(one_hot(hids, t.shape[0]), t).astype(BF))(history)
    g0, g1 = by_part(looked, swap(looked))

    def split(t, i):
        own = t[:rows]
        side = [t[rows + k * edge : rows + (k + 1) * edge] for k in range(4)]
        hist = t[rows + 4 * edge : -16]
        send = [one_hot(i[k * edge : (k + 1) * edge], rows) for k in range(4)]
        return own, side, hist, send

    own0, side0, hist0, send0 = split(t0, i0)
    own1, side1, hist1, send1 = split(t1, i1)
    q10 = dot_t(side1[0], send0[0]).astype(BF)
    q01 = dot_t(side0[1], send1[1]).astype(BF)
    near = jnp.concatenate(
        [jnp.concatenate([own0, q01], axis=1), jnp.concatenate([q10, own1], axis=1)], axis=0
    )
    zs = jnp.zeros_like(side0[0])
    from_before = jnp.concatenate(
        [
            jnp.concatenate([side0[0], side0[2], zs], axis=0),
            jnp.concatenate([zs, zs, side1[2]], axis=0),
        ],
        axis=1,
    )
    from_after = jnp.concatenate(
        [
            jnp.concatenate([side0[3], zs, zs], axis=0),
            jnp.concatenate([zs, side1[1], side1[3]], axis=0),
        ],
        axis=1,
    )
    to_after = jnp.concatenate(
        [
            jnp.concatenate([zs, send1[0]], axis=1),
            jnp.concatenate([send0[2], zs], axis=1),
            jnp.concatenate([zs, send1[2]], axis=1),
        ],
        axis=0,
    )
    to_before = jnp.concatenate(
        [
            jnp.concatenate([send0[3], zs], axis=1),
            jnp.concatenate([send0[1], zs], axis=1),
            jnp.concatenate([zs, send1[3]], axis=1),
        ],
        axis=0,
    )
    far_a = jnp.where(chip_odd == 0, from_after, from_before)
    far_b = jnp.where(chip_odd == 0, from_before, from_after)
    pick_a = jnp.where(chip_odd == 0, to_after, to_before)
    pick_b = jnp.where(chip_odd == 0, to_before, to_after)
    zh = jnp.zeros_like(hist0)
    hist_t = jnp.concatenate(
        [jnp.concatenate([hist0, zh], axis=1), jnp.concatenate([zh, hist1], axis=1)], axis=0
    )
    looked = jnp.concatenate([g0, g1], axis=1)
    start = jnp.concatenate([x0, x1], axis=0)

    far = jnp.concatenate([far_a, far_b], axis=0).T
    picks = jnp.concatenate([pick_a, pick_b], axis=0)
    hist_n = hist_t.T
    current = start
    sent = dot(picks, current).astype(BF)
    send_a, send_b = sent[: 3 * edge], sent[3 * edge :]
    place = core.astype(jnp.int32).reshape(1)
    early = [early_weight(0, None)[0]]
    for layer in range(1, EARLY):
        arriving, early[-1] = early_weight(layer, early[-1])
        early.append(arriving)
    held, early[0] = lax.optimization_barrier((current, early[0]))
    (local,) = begin(None, held, near, hist_n, looked[0], None)
    weight = None
    own_rows = []
    for layer in range(layers):
        got_b = exchange(send_b, 2)
        got_a = exchange(send_a, 0)
        if layer < EARLY:
            mine = half_finish(layer, place, local, got_a, got_b, far, start, early[layer])
            current, send_a, send_b = join(place, mine, swap(mine), picks)
        else:
            current, send_a, send_b = finish(
                layer, local, got_a, got_b, far, picks, start, weight
            )
        if layer + 1 < layers:
            brought = layer + 1 - EARLY if layer + 1 >= EARLY else None
            held = current
            if layer + 1 < EARLY:
                held, early[layer + 1] = lax.optimization_barrier((current, early[layer + 1]))
            out = begin(brought, held, near, hist_n, looked[layer + 1], resident)
            local, weight = (out[0], None) if brought is None else out
        own_rows.append(lax.dynamic_slice_in_dim(current, core * rows, rows, 0))
    whole = jnp.stack(own_rows)
    return lax.all_to_all(whole, "segment", 0, 1, tiled=True)


def solution(mesh):
    in_specs = (
        P("graph", None),
        P(None, "graph", None),
        P(None, "graph", None),
        P(None, "graph", None),
        P(None, None, "graph", None),
        P(None, "graph", None),
        P(None, None, "graph"),
        P(None, "graph"),
    )
    out_specs = P("segment", "graph", None)
    return jax.shard_map(shards, mesh=mesh, in_specs=in_specs, out_specs=out_specs, check_vma=False)
```
